768 devices in a mesh: seq: 16 (over y, core), cp: 48 (over z, x).
Axes of the slice: x: 4, y: 8, z: 12, core: 2. Of those that a mesh axis runs over, the one named last changes fastest.
Arguments:
- query: bfloat16 [98304, 4608], P(('seq', 'cp')), may hold values from -6 to 6
- key_proj: bfloat16 [98304, 4608], P(('seq', 'cp')), may hold values from -6 to 6
- value_proj: bfloat16 [98304, 4608], P(('seq', 'cp')), may hold values from -6 to 6
- featurizer: float32 [3, 7, 288], replicated, may hold values from -2 to 2
- rates: float32 [16, 4608], replicated, may hold values from 2.5431316e-06 to 0.25
- residues: float32 [16, 4608], replicated, may hold values from -5 to 5
- skip: float32 [4608], replicated, may hold values from -4 to 4
Outputs:
- operator_out: bfloat16 [98304, 4608], P(('seq', 'cp'))
The draws below stay inside these ranges and needn't reach their ends.
All inputs are finite; a program needn't handle non-finite values.
Results may differ from the reference program's by a relative error of at most 0.0064.
Values may be sent and summed in bfloat16 or wider, within the bound.
A program may use at most 128 MiB of HBM per device.

```python
import math
import jax
import jax.numpy as jnp
from jax import lax

DW = 4608
TAPS = 7
MODES = 16
NGROUPS = 288
TOKENS = 98304


def steps_of(rng, shape, split, smallest, largest):
    gain = 1.0
    for axis_at, shards_of in split:
        steps = jax.random.uniform(jax.random.fold_in(jax.random.fold_in(rng, 6), axis_at), (shards_of,), jnp.float32, smallest / len(split), largest / len(split))
        gain = gain * jnp.repeat(jnp.exp(steps), shape[axis_at] // shards_of).reshape((-1,) + (1,) * (len(shape) - 1 - axis_at))
    return gain


def bell_draw(key, extent, width, limit, cuts=(), kind=jnp.bfloat16):
    entries = jax.random.normal(key, extent, jnp.float32) * width
    if len(cuts) > 0:
        entries = steps_of(key, extent, cuts, -0.22, 0.18) * entries
    return jnp.clip(entries, min=-limit, max=limit).astype(kind)


def setup_inputs(seed: int = 0) -> dict:
    keys = jax.random.split(jax.random.key(seed), 8)
    query = bell_draw(keys[0], (TOKENS, DW), 1.0, 6.0, ((0, 768),))
    key_proj = bell_draw(keys[1], (TOKENS, DW), 1.0, 6.0, ((0, 768),))
    value_proj = bell_draw(keys[2], (TOKENS, DW), 1.0, 6.0, ((0, 768),))
    featurizer = bell_draw(keys[3], (3, TAPS, NGROUPS), TAPS ** -0.5, 2.0, (), jnp.float32)
    rates = jnp.clip(jnp.exp(jax.random.uniform(keys[4], (MODES, DW), jnp.float32, math.log(2.543131586207892e-06), math.log(0.25))), 2.543131586207892e-06, 0.25)
    residues = bell_draw(keys[5], (MODES, DW), 1.0, 5.0, (), jnp.float32)
    skip = bell_draw(keys[6], (DW,), 1.0, 4.0, (), jnp.float32)
    return {"query": query, "key_proj": key_proj, "value_proj": value_proj, "featurizer": featurizer, "rates": rates, "residues": residues, "skip": skip}


precise = lax.Precision.HIGHEST

def mode_terms(decay_rate, residue_part):
    mode_count = decay_rate.shape[1]
    return residue_part * jnp.sqrt(-jnp.expm1(-2.0 * decay_rate) / mode_count)

def short_conv(extended, tap_table, row_count):
    tap_count = tap_table.shape[0]
    running = jnp.zeros((row_count, extended.shape[1]), jnp.float32)
    for lag_index in range(tap_count):
        first_row = tap_count - 1 - lag_index
        running = running + tap_table[lag_index][None, :] * extended[first_row:first_row + row_count].astype(jnp.float32)
    return running

def link_blocks(earlier, later):
    return (earlier[0] * later[0], later[0] * earlier[1] + later[1])

def modal_local(signal, decay_rate, mode_coef, block_len):
    row_count, chan_count = signal.shape
    block_count = row_count // block_len
    blocks = signal.reshape(block_count, block_len, chan_count)
    offsets = jnp.arange(block_len, dtype=jnp.float32)
    falloff = jnp.exp(-decay_rate[None, :, :] * offsets[:, None, None])
    kernel = lax.optimization_barrier(jnp.sum(mode_coef[None] * falloff, axis=2))
    lag_table = jnp.arange(block_len, dtype=jnp.int32)[:, None] - jnp.arange(block_len, dtype=jnp.int32)[None, :]
    toeplitz = jnp.where((lag_table >= 0)[:, :, None], kernel[jnp.maximum(lag_table, 0)], 0.0)
    within = jnp.einsum('ijc,bjc->bic', toeplitz, blocks, precision=precise)
    block_state = jnp.einsum('jcr,bjc->bcr', falloff[::-1], blocks, precision=precise)
    factor = jnp.broadcast_to(jnp.exp(-decay_rate * block_len)[None], block_state.shape)
    _, through = lax.associative_scan(link_blocks, (factor, block_state))
    entering = jnp.concatenate([jnp.zeros_like(through[:1]), through[:-1]], axis=0)
    leading = mode_coef[None] * falloff * jnp.exp(-decay_rate)[None]
    carried = jnp.einsum('icr,bcr->bic', leading, entering, precision=precise)
    return ((within + carried).reshape(row_count, chan_count), through[-1])

def reference(query, key_proj, value_proj, featurizer, rates, residues, skip):
    row_count, feature_width = query.shape
    tap_count = featurizer.shape[1]
    filters = jnp.repeat(featurizer, feature_width // featurizer.shape[2], axis=2)
    chan_block = math.gcd(feature_width, 128)
    block_total = feature_width // chan_block

    def per_block(block_index):
        col_start = block_index * chan_block
        tap_part = lax.dynamic_slice_in_dim(filters, col_start, chan_block, 2)
        featured = []
        for member, source in enumerate((query, key_proj, value_proj)):
            columns = lax.dynamic_slice_in_dim(source, col_start, chan_block, 1)
            extended = jnp.concatenate([jnp.zeros((tap_count - 1, chan_block), columns.dtype), columns], axis=0)
            featured.append(short_conv(extended, tap_part[member], row_count))
        gate_half = featured[0].astype(jnp.bfloat16)
        gate = lax.optimization_barrier(gate_half).astype(jnp.float32)
        signal_half = (featured[1] * featured[2]).astype(jnp.bfloat16)
        signal = lax.optimization_barrier(signal_half).astype(jnp.float32)
        decay_rate = lax.dynamic_slice_in_dim(rates, col_start, chan_block, 1).T
        residue_part = lax.dynamic_slice_in_dim(residues, col_start, chan_block, 1).T
        mode_coef = mode_terms(decay_rate, residue_part)
        convolved, _ = modal_local(signal, decay_rate, mode_coef, 16)
        skip_part = lax.dynamic_slice_in_dim(skip, col_start, chan_block, 0)
        convolved = convolved + skip_part[None, :] * signal
        conv_half = lax.optimization_barrier(convolved.astype(jnp.bfloat16))
        return (gate * conv_half.astype(jnp.float32)).astype(jnp.bfloat16)
    stacked = lax.map(per_block, jnp.arange(block_total, dtype=jnp.int32))
    return stacked.transpose(1, 0, 2).reshape(row_count, feature_width)
```

```python
import functools

import jax
import jax.numpy as jnp
from jax import lax
from jax.experimental import pallas as pl
from jax.experimental.pallas import tpu as pltpu
from jax.sharding import PartitionSpec as P

F32 = jnp.float32
BF16 = jnp.bfloat16
LANES = 128
SUBS = 8
ROWS = 128
STEPS = ROWS // SUBS
MESH = pl.DeviceIdType.MESH


def rounded(value):
    return value.astype(BF16).astype(F32)


def kernel(
    nx, nz, ns, taps_n, modes, tiles,
    q_hbm, k_hbm, v_hbm, taps, rates, coef, skip, out,
    raw, halo, ext, perm, u, y, gate, sx, ends, rx, pre, rowsum, rz, prez, tot, ry, bsend, base, xsend, enter,
    in_sem, hs_sem, hr_sem, xs_sem, xr_sem, zs_sem, zr_sem, ys_sem, yr_sem, bs_sem, br_sem, ws_sem, wr_sem, own_sem,
):
    quarter = tiles // nx
    seq = lax.axis_index("seq")
    cp = lax.axis_index("cp")
    z = cp // nx
    x = cp % nx
    linear = seq * (nx * nz) + cp
    count = nx * nz * ns
    sub = lax.broadcasted_iota(jnp.int32, (SUBS, LANES), 0)

    def device(seq_at, cp_at):
        return {"seq": seq_at, "cp": cp_at}

    after = lax.rem(linear + 1, count)
    before = lax.rem(linear + count - 1, count)
    after_dev = device(after // (nx * nz), after % (nx * nz))
    before_dev = device(before // (nx * nz), before % (nx * nz))

    def at_x(step):
        return device(seq, z * nx + lax.rem(x + step, nx))

    def at_z(step):
        return device(seq, lax.rem(z + step, nz) * nx + x)

    def at_s(step):
        return device(lax.rem(seq + step, ns), cp)

    sources = (q_hbm, k_hbm, v_hbm)
    loads = [pltpu.make_async_copy(sources[m], raw.at[m], in_sem.at[m]) for m in range(3)]
    for m in (1, 2, 0):
        loads[m].start()

    barrier = pltpu.get_barrier_semaphore()
    for target in (after_dev, before_dev):
        pl.semaphore_signal(barrier, inc=1, device_id=target, device_id_type=MESH)
    for step in range(1, nx):
        pl.semaphore_signal(barrier, inc=1, device_id=at_x(step), device_id_type=MESH)

    def greet_z(step, carry):
        pl.semaphore_signal(barrier, inc=1, device_id=at_z(step), device_id_type=MESH)
        return carry

    def greet_s(step, carry):
        pl.semaphore_signal(barrier, inc=1, device_id=at_s(step), device_id_type=MESH)
        return carry

    lax.fori_loop(1, nz, greet_z, 0)
    lax.fori_loop(1, ns, greet_s, 0)
    pl.semaphore_wait(barrier, 2 + (nx - 1) + (nz - 1) + (ns - 1))

    def halo_copy(m):
        return pltpu.make_async_remote_copy(
            src_ref=sources[m].at[pl.ds(ROWS - SUBS, SUBS), :],
            dst_ref=halo.at[m],
            send_sem=hs_sem.at[m],
            recv_sem=hr_sem.at[m],
            device_id=after_dev,
            device_id_type=MESH,
        )

    for m in (1, 2, 0):
        halo_copy(m).start()

    seen = (linear > 0).astype(F32)

    def lanes_of(tile):
        return pl.ds(pl.multiple_of(tile * LANES, LANES), LANES)

    def row(ref, index, lanes):
        return jnp.broadcast_to(ref[index:index + 1, lanes], (SUBS, LANES))

    def featured(m, lanes):
        ext[m, 0:SUBS, :] = halo[m, :, lanes].astype(F32) * seen
        ext[m, SUBS:SUBS + ROWS, :] = raw[m, :, lanes].astype(F32)
        shifted = {
            j: ext[m, pl.ds(SUBS + j, SUBS, stride=STEPS), :] for j in range(1 - taps_n, STEPS)
        }
        weights = [
            jnp.broadcast_to(taps[m, i:i + 1, lanes], (SUBS, LANES)) for i in range(taps_n)
        ]
        result = []
        for j in range(STEPS):
            total = weights[0] * shifted[j]
            for i in range(1, taps_n):
                total = total + weights[i] * shifted[j - i]
            result.append(total)
        return result

    for m in (1, 2):
        loads[m].wait()
        halo_copy(m).wait_recv()

    def first(tile, carry):
        lanes = lanes_of(tile)
        part = tile // quarter
        inner = lanes_of(tile % quarter)
        key = featured(1, lanes)
        value = featured(2, lanes)
        signal = [rounded(key[j] * value[j]) for j in range(STEPS)]
        for j in range(STEPS):
            u[j * SUBS:(j + 1) * SUBS, lanes] = signal[j]
        decay_all = jnp.exp(-rates[:, lanes])
        for r in range(modes):
            a = jnp.broadcast_to(decay_all[r:r + 1], (SUBS, LANES))
            s = signal[0]
            for j in range(1, STEPS):
                s = s * a + signal[j]
            a2 = a * a
            a4 = a2 * a2
            a8 = a4 * a4
            a16 = a8 * a8
            a32 = a16 * a16
            a64 = a32 * a32
            s = s + jnp.where(sub >= 1, a16 * pltpu.roll(s, 1, 0), 0.0)
            s = s + jnp.where(sub >= 2, a32 * pltpu.roll(s, 2, 0), 0.0)
            s = s + jnp.where(sub >= 4, a64 * pltpu.roll(s, 4, 0), 0.0)
            ends[part, r:r + 1, inner] = s[SUBS - 1:SUBS]
            sx[r, :, lanes] = jnp.where(sub >= 1, pltpu.roll(s, 1, 0), 0.0)
        return carry

    lax.fori_loop(0, tiles, first, 0)

    def x_copy(step):
        return pltpu.make_async_remote_copy(
            src_ref=ends.at[lax.rem(x + step, nx)],
            dst_ref=rx.at[step],
            send_sem=xs_sem.at[step],
            recv_sem=xr_sem.at[step],
            device_id=at_x(step),
            device_id_type=MESH,
        )

    for step in range(1, nx):
        x_copy(step).start()
    own = pltpu.make_async_copy(ends.at[x], rx.at[0], own_sem.at[0])
    own.start()

    def second(tile, carry):
        lanes = lanes_of(tile)
        query = featured(0, lanes)
        for j in range(STEPS):
            gate[j * SUBS:(j + 1) * SUBS, lanes] = rounded(query[j])
        decay_all = jnp.exp(-rates[:, lanes])
        power = coef[:, lanes]
        tap = []
        for j in range(STEPS):
            tap.append(jnp.broadcast_to(jnp.sum(power, axis=0, keepdims=True), (SUBS, LANES)))
            power = power * decay_all
        tap[0] = tap[0] + jnp.broadcast_to(skip[:, lanes], (SUBS, LANES))
        signal = [u[j * SUBS:(j + 1) * SUBS, lanes] for j in range(STEPS)]
        for j in range(STEPS):
            total = tap[0] * signal[j]
            for i in range(1, j + 1):
                total = total + tap[i] * signal[j - i]
            y[j * SUBS:(j + 1) * SUBS, lanes] = total
        return carry

    loads[0].wait()
    halo_copy(0).wait_recv()
    lax.fori_loop(0, tiles, second, 0)

    own.wait()
    for step in range(1, nx):
        x_copy(step).wait_recv()

    def slot(position, place, size):
        return lax.rem(place - position + size, size)

    def row_prefix(tile, carry):
        lanes = lanes_of(tile)
        rate = rates[:, lanes_of(x * quarter + tile)]
        factor = jnp.exp(-rate * float(ROWS))
        state = rx[slot(0, x, nx), :, lanes]
        for i in range(1, nx):
            pre[i, :, lanes] = state
            state = factor * state + rx[slot(i, x, nx), :, lanes]
        rowsum[tile] = state
        return carry

    lax.fori_loop(0, quarter, row_prefix, 0)

    owner = z < quarter
    my_tile = lanes_of(x * quarter + lax.rem(z, quarter))

    def z_copy(step):
        return pltpu.make_async_remote_copy(
            src_ref=rowsum.at[lax.rem(lax.rem(z + step, nz), quarter)],
            dst_ref=rz.at[step],
            send_sem=zs_sem.at[step],
            recv_sem=zr_sem.at[step],
            device_id=at_z(step),
            device_id_type=MESH,
        )

    def z_sends(step):
        return lax.rem(z + step, nz) < quarter

    def z_start(step, carry):
        @pl.when(z_sends(step))
        def _():
            z_copy(step).start()
        return carry

    lax.fori_loop(1, nz, z_start, 0)

    def b_copy(step):
        return pltpu.make_async_remote_copy(
            src_ref=bsend.at[lax.rem(z + step, nz)],
            dst_ref=base.at[lax.rem(z, quarter)],
            send_sem=bs_sem.at[step],
            recv_sem=br_sem.at[step],
            device_id=at_z(step),
            device_id_type=MESH,
        )

    def y_copy(step):
        return pltpu.make_async_remote_copy(
            src_ref=tot,
            dst_ref=ry.at[step],
            send_sem=ys_sem.at[step],
            recv_sem=yr_sem.at[step],
            device_id=at_s(step),
            device_id_type=MESH,
        )

    @pl.when(owner)
    def _():
        rate = rates[:, my_tile]
        row_factor = jnp.exp(-rate * float(ROWS * nx))
        group_factor = jnp.exp(-rate * float(ROWS * nx * nz))
        rz[0] = rowsum[lax.rem(z, quarter)]

        def z_wait(step, carry):
            z_copy(step).wait_recv()
            return carry

        lax.fori_loop(1, nz, z_wait, 0)

        def z_join(i, state):
            prez[i] = state
            return row_factor * state + rz[slot(i, z, nz)]

        tot[...] = lax.fori_loop(0, nz, z_join, jnp.zeros((modes, LANES), F32))

        def y_start(step, carry):
            @pl.when(seq + step < ns)
            def _():
                y_copy(step).start()
            return carry

        lax.fori_loop(1, ns, y_start, 0)

        def y_wait(step, carry):
            y_copy(step).wait_recv()
            return carry

        lax.fori_loop(1, seq + 1, y_wait, 0)

        def y_join(i, state):
            return group_factor * state + ry[seq - i]

        group = lax.fori_loop(0, seq, y_join, jnp.zeros((modes, LANES), F32))

        def b_make(i, grown):
            bsend[i] = prez[i] + grown
            return grown * row_factor

        lax.fori_loop(0, nz, b_make, group)
        base[lax.rem(z, quarter)] = bsend[z]

        def b_start(step, carry):
            b_copy(step).start()
            return carry

        lax.fori_loop(1, nz, b_start, 0)

    def b_comes(step):
        return lax.rem(z - step + nz, nz) < quarter

    def b_wait(step, carry):
        @pl.when(b_comes(step))
        def _():
            b_copy(step).wait_recv()
        return carry

    lax.fori_loop(1, nz, b_wait, 0)

    def spread(tile, carry):
        lanes = lanes_of(tile)
        rate = rates[:, lanes_of(x * quarter + tile)]
        factor = jnp.exp(-rate * float(ROWS))
        grown = base[tile]
        xsend[0, :, lanes] = grown
        for i in range(1, nx):
            grown = grown * factor
            xsend[i, :, lanes] = pre[i, :, lanes] + grown
        return carry

    lax.fori_loop(0, quarter, spread, 0)

    def w_copy(step):
        return pltpu.make_async_remote_copy(
            src_ref=xsend.at[lax.rem(x + step, nx)],
            dst_ref=enter.at[x],
            send_sem=ws_sem.at[step],
            recv_sem=wr_sem.at[step],
            device_id=at_x(step),
            device_id_type=MESH,
        )

    for step in range(1, nx):
        w_copy(step).start()
    own_back = pltpu.make_async_copy(xsend.at[x], enter.at[x], own_sem.at[1])
    own_back.start()
    own_back.wait()
    for step in range(1, nx):
        w_copy(step).wait_recv()

    def third(tile, carry):
        lanes = lanes_of(tile)
        part = tile // quarter
        inner = lanes_of(tile % quarter)
        decay_all = jnp.exp(-rates[:, lanes])
        lead_all = coef[:, lanes] * decay_all
        enter_all = enter[part, :, inner]
        acc = [y[j * SUBS:(j + 1) * SUBS, lanes] for j in range(STEPS)]
        for r in range(modes):
            a = jnp.broadcast_to(decay_all[r:r + 1], (SUBS, LANES))
            a2 = a * a
            a4 = a2 * a2
            a8 = a4 * a4
            a16 = a8 * a8
            a32 = a16 * a16
            a64 = a32 * a32
            grow = (
                jnp.where(sub % 2 == 1, a16, 1.0)
                * jnp.where((sub // 2) % 2 == 1, a32, 1.0)
                * jnp.where(sub >= 4, a64, 1.0)
            )
            g = sx[r, :, lanes] + grow * jnp.broadcast_to(enter_all[r:r + 1], (SUBS, LANES))
            g = g * jnp.broadcast_to(lead_all[r:r + 1], (SUBS, LANES))
            for j in range(STEPS):
                acc[j] = acc[j] + g
                if j + 1 < STEPS:
                    g = g * a
        for j in range(STEPS):
            product = gate[j * SUBS:(j + 1) * SUBS, lanes] * rounded(acc[j])
            perm[pl.ds(j, SUBS, stride=STEPS), :] = product
        out[:, lanes] = perm[...].astype(BF16)
        return carry

    lax.fori_loop(0, tiles, third, 0)

    for m in range(3):
        halo_copy(m).wait_send()
    for step in range(1, nx):
        x_copy(step).wait_send()
        w_copy(step).wait_send()

    def z_drain(step, carry):
        @pl.when(z_sends(step))
        def _():
            z_copy(step).wait_send()
        return carry

    lax.fori_loop(1, nz, z_drain, 0)

    @pl.when(owner)
    def _():
        def b_drain(step, carry):
            b_copy(step).wait_send()
            return carry

        lax.fori_loop(1, nz, b_drain, 0)

        def y_drain(step, carry):
            @pl.when(seq + step < ns)
            def _():
                y_copy(step).wait_send()
            return carry

        lax.fori_loop(1, ns, y_drain, 0)


def local(nx, nz, ns, query, key_proj, value_proj, featurizer, rates, residues, skip):
    row_count, width = query.shape
    taps_n = featurizer.shape[1]
    modes = rates.shape[0]
    tiles = width // LANES
    quarter = tiles // nx
    taps = jnp.repeat(featurizer, width // featurizer.shape[2], axis=2)
    coef = residues * jnp.sqrt(-jnp.expm1(-2.0 * rates) / modes)
    vm = pltpu.VMEM
    dma = pltpu.SemaphoreType.DMA
    any_spec = pl.BlockSpec(memory_space=pl.ANY)
    vmem_spec = pl.BlockSpec(memory_space=pltpu.VMEM)
    part = quarter * LANES
    return pl.pallas_call(
        functools.partial(kernel, nx, nz, ns, taps_n, modes, tiles),
        out_shape=jax.ShapeDtypeStruct((row_count, width), BF16),
        in_specs=[any_spec] * 3 + [vmem_spec] * 4,
        out_specs=vmem_spec,
        scratch_shapes=[
            vm((3, row_count, width), BF16),
            vm((3, SUBS, width), BF16),
            vm((3, SUBS + row_count, LANES), F32),
            vm((row_count, LANES), F32),
            vm((row_count, width), F32),
            vm((row_count, width), F32),
            vm((row_count, width), F32),
            vm((modes, SUBS, width), F32),
            vm((nx, modes, part), F32),
            vm((nx, modes, part), F32),
            vm((nx, modes, part), F32),
            vm((quarter, modes, LANES), F32),
            vm((nz, modes, LANES), F32),
            vm((nz, modes, LANES), F32),
            vm((modes, LANES), F32),
            vm((ns, modes, LANES), F32),
            vm((nz, modes, LANES), F32),
            vm((quarter, modes, LANES), F32),
            vm((nx, modes, part), F32),
            vm((nx, modes, part), F32),
            dma((3,)),
            dma((3,)),
            dma((3,)),
            dma((nx,)),
            dma((nx,)),
            dma((nz,)),
            dma((nz,)),
            dma((ns,)),
            dma((ns,)),
            dma((nz,)),
            dma((nz,)),
            dma((nx,)),
            dma((nx,)),
            dma((2,)),
        ],
        compiler_params=pltpu.CompilerParams(
            collective_id=0, has_side_effects=True, vmem_limit_bytes=48 << 20
        ),
    )(query, key_proj, value_proj, taps, rates, coef, skip.reshape(1, width))


def solution(mesh):
    nx = 4
    ns = mesh.shape["seq"]
    nz = mesh.shape["cp"] // nx
    rows = P(("seq", "cp"), None)
    return jax.shard_map(
        functools.partial(local, nx, nz, ns),
        mesh=mesh,
        in_specs=(rows, rows, rows, P(), P(), P(), P()),
        out_specs=rows,
        check_vma=False,
    )
```
